128 devices in a mesh: seq: 8 (over x, core), chan: 16 (over y, z).
Axes of the slice: x: 4, y: 4, z: 4, core: 2. Of those that a mesh axis runs over, the one named last changes fastest.
Arguments:
- tokens: bfloat16 [6144, 8192], P('seq', 'chan'), may hold values from -6 to 6
- norm_gain: bfloat16 [8192], P('chan'), may hold values from 0.099609375 to 1.8984375
- in_weight: bfloat16 [8192, 3, 8192], P('seq', None, 'chan'), may hold values from -0.0625 to 0.0625
- conv_weight: bfloat16 [3, 3, 8192], P(None, None, 'chan'), may hold values from -3 to 3
- filters: bfloat16 [512, 128], P('chan'), may hold values from -0.5 to 0.5
- out_weight: bfloat16 [8192, 8192], P('chan'), may hold values from -0.09375 to 0.09375
Outputs:
- result: bfloat16 [6144, 8192], P('seq', 'chan')
The draws below stay inside these ranges and needn't reach their ends.
All inputs are finite; a program needn't handle non-finite values.
Results may differ from the reference program's by a relative error of at most 0.0084.
Values may be sent and summed in bfloat16 or wider, within the bound.
A program may use at most 192 MiB of HBM per device.

```python
import jax
import jax.numpy as jnp
import numpy as np
from jax import lax

D = 8192
FILT = 128
TOKENS = 6144
GROUPS = 512


def with_spikes(array, stream_key, source, target, shards_of, factor):
    owner, partner = [(jnp.arange(array.shape[position]) // (array.shape[position] // shards_of)).reshape([-1 if axis == position else 1 for axis in range(array.ndim)]) for position in (source, target)]
    chosen = jax.random.permutation(stream_key, shards_of)[partner]
    strong = (owner == chosen) | (owner == (partner + shards_of // 2) % shards_of)
    return jnp.where(strong, factor * array, array)


def steps_of(own_key, extent, shards, low, high):
    factor_of, own = 1.0, jax.random.fold_in(own_key, 6)
    for position, shards_of in shards:
        heights = jnp.exp(jax.random.uniform(jax.random.fold_in(own, position), (shards_of,), jnp.float32, low / len(shards), high / len(shards)))
        factor_of = factor_of * jnp.repeat(heights, extent[position] // shards_of).reshape([-1 if axis == position else 1 for axis in range(len(extent))])
    return factor_of


def scatter_about(own_key, dims, spread, bound, cuts=(), kind=jnp.bfloat16):
    array = jax.random.normal(own_key, dims, jnp.float32) * spread
    if len(cuts) > 0:
        array = steps_of(own_key, dims, cuts, -0.22, 0.18) * array
    return jnp.clip(array, min=-bound, max=bound).astype(kind)


def heavy_noise(own_key, dims, deviation, most, pieces, heavy, kind=jnp.bfloat16):
    drawn = deviation * jax.random.normal(own_key, dims, jnp.float32)
    if pieces:
        drawn = drawn * steps_of(own_key, dims, pieces, -0.22, 0.18)
    return jnp.clip(with_spikes(drawn, jax.random.fold_in(own_key, 3), *heavy), -most, most).astype(kind)


def setup_inputs(seed: int = 0) -> dict:
    arg_keys = jax.random.split(jax.random.key(seed), 7)
    tokens = scatter_about(arg_keys[0], (TOKENS, D), 1.0, 6.0, ((0, 8), (1, 16)))
    norm_gain = jnp.clip(1.0 + 0.18 * jax.random.normal(arg_keys[1], (D,), jnp.float32), 0.099609375, 1.8984375).astype(jnp.bfloat16)
    in_weight = scatter_about(arg_keys[2], (D, 3, D), D ** -0.5, 0.0625, ((0, 8), (2, 16)))
    conv_weight = scatter_about(arg_keys[3], (3, 3, D), 0.6, 3.0, ((2, 16),))
    filters = scatter_about(arg_keys[4], (GROUPS, FILT), FILT ** -0.5, 0.5, ((0, 16),))
    out_weight = heavy_noise(arg_keys[5], (D, D), D ** -0.5, 0.09375, ((0, 16),), (0, 1, 16, 2.0))
    return dict(tokens=tokens, norm_gain=norm_gain, in_weight=in_weight, conv_weight=conv_weight, filters=filters, out_weight=out_weight)


def lag_tables(filters):
    length = filters.shape[1]
    offsets = np.arange(length)[:, None] - np.arange(length)[None, :]
    lookup = filters[:, offsets % length]
    lower = jnp.asarray(offsets >= 0)
    zero_value = jnp.zeros((), filters.dtype)
    return (jnp.where(lower, lookup, zero_value), jnp.where(lower, zero_value, lookup))

def hyena_core(extended, conv_weight, filters):
    length = filters.shape[1]
    values = extended.astype(jnp.float32)
    weights = conv_weight.astype(jnp.float32)
    shaped = weights[:, 0, :] * values[2:] + weights[:, 1, :] * values[1:-1] + weights[:, 2, :] * values[:-2]
    total = shaped.shape[0]
    out_rows = total - length
    query = shaped[length:, 0, :]
    mixed = (shaped[:, 1, :] * shaped[:, 2, :]).astype(jnp.bfloat16)
    group_count = filters.shape[0]
    channel_count = mixed.shape[1]
    blocks = mixed.reshape(total // length, length, group_count, channel_count // group_count).astype(jnp.float32)
    now_table, prev_table = lag_tables(filters)
    filtered = jnp.einsum('gts,bsgw->btgw', now_table.astype(jnp.float32), blocks[1:], precision=lax.Precision.HIGHEST)
    filtered = filtered + jnp.einsum('gts,bsgw->btgw', prev_table.astype(jnp.float32), blocks[:-1], precision=lax.Precision.HIGHEST)
    filtered = filtered.reshape(out_rows, channel_count)
    return (query * filtered).astype(jnp.bfloat16)

def reference(tokens, norm_gain, in_weight, conv_weight, filters, out_weight):
    values = tokens.astype(jnp.float32)
    mean_square = lax.optimization_barrier(jnp.mean(values * values, axis=1, keepdims=True))
    normed = (values * lax.rsqrt(mean_square + 1e-06) * norm_gain.astype(jnp.float32)).astype(jnp.bfloat16)
    streams = jnp.dot(normed, in_weight.reshape(D, 3 * D), preferred_element_type=jnp.float32)
    streams = streams.astype(jnp.bfloat16).reshape(TOKENS, 3, D)
    padding = jnp.zeros((FILT + 2, 3, D), jnp.bfloat16)
    gated = hyena_core(jnp.concatenate([padding, streams], axis=0), conv_weight, filters)
    branch = jnp.dot(gated, out_weight, preferred_element_type=jnp.float32)
    return (values + branch).astype(jnp.bfloat16)
```

```python
import jax
import jax.numpy as jnp
import numpy as np
from jax import lax
from jax.sharding import PartitionSpec as P


def lag_table(filters):
    groups, length = filters.shape
    width = 3 * length
    zeros = jnp.zeros((groups, length), filters.dtype)
    skew = jnp.concatenate([zeros, filters[:, ::-1], zeros], axis=1)
    tiled = jnp.tile(skew, (1, length + 1))[:, : length * (width + 1)]
    windows = tiled.reshape(groups, length, width + 1)[:, :, : 2 * length]
    return windows[:, ::-1, :]


def hyena_core(extended, conv_weight, filters):
    length = filters.shape[1]
    values = extended.astype(jnp.float32)
    weights = conv_weight.astype(jnp.float32)
    shaped = (
        weights[:, 0, :] * values[2:]
        + weights[:, 1, :] * values[1:-1]
        + weights[:, 2, :] * values[:-2]
    )
    total = shaped.shape[0]
    out_rows = total - length
    query = shaped[length:, 0, :]
    mixed = (shaped[:, 1, :] * shaped[:, 2, :]).astype(jnp.bfloat16)
    group_count = filters.shape[0]
    channel_count = mixed.shape[1]
    blocks = mixed.reshape(total // length, length, group_count, channel_count // group_count)
    paired = jnp.concatenate([blocks[:-1], blocks[1:]], axis=1)
    table = lag_table(filters)
    filtered = jnp.einsum(
        "gts,bsgw->btgw", table, paired, preferred_element_type=jnp.float32
    )
    filtered = filtered.reshape(out_rows, channel_count)
    return (query * filtered).astype(jnp.bfloat16)


def local(tokens, norm_gain, in_weight, conv_weight, filters, out_weight):
    row_count = tokens.shape[0]
    chan_count = in_weight.shape[2]
    length = filters.shape[1]
    joined = jnp.concatenate([tokens, norm_gain[None, :]], axis=0)
    whole_joined = lax.all_gather(joined, "chan", axis=1, tiled=True)
    whole, gain_whole = whole_joined[:row_count], whole_joined[row_count]
    values = whole.astype(jnp.float32)
    mean_square = jnp.mean(values * values, axis=1, keepdims=True)
    normed = (values * lax.rsqrt(mean_square + 1e-06) * gain_whole.astype(jnp.float32)).astype(
        jnp.bfloat16
    )
    piece = lax.all_gather(in_weight, "seq", axis=0, tiled=True)
    panel = piece.reshape(piece.shape[0], 3 * chan_count)
    projected = jnp.dot(normed, panel, preferred_element_type=jnp.float32)
    streams = projected.astype(jnp.bfloat16).reshape(row_count, 3, chan_count)
    parts_count = lax.axis_size("seq")
    halo_rows = length + 2
    shift = [(i, i + 1) for i in range(parts_count - 1)]
    halo = lax.ppermute(streams[row_count - halo_rows :], "seq", shift)
    extended = jnp.concatenate([halo, streams], axis=0)
    gated = hyena_core(extended, conv_weight, filters)
    partial_out = jnp.dot(gated, out_weight, preferred_element_type=jnp.float32)
    summed = lax.psum_scatter(partial_out, "chan", scatter_dimension=1, tiled=True)
    return (tokens.astype(jnp.float32) + summed).astype(jnp.bfloat16)


def solution(mesh):
    return jax.shard_map(
        local,
        mesh=mesh,
        in_specs=(
            P("seq", "chan"),
            P("chan"),
            P("seq", None, "chan"),
            P(None, None, "chan"),
            P("chan", None),
            P("chan", None),
        ),
        out_specs=P("seq", "chan"),
        check_vma=False,
    )
```

```python
import jax
import jax.numpy as jnp
import numpy as np
from jax import lax
from jax.sharding import PartitionSpec as P


def lag_table(filters):
    groups, length = filters.shape
    width = 3 * length
    zeros = jnp.zeros((groups, length), filters.dtype)
    skew = jnp.concatenate([zeros, filters[:, ::-1], zeros], axis=1)
    tiled = jnp.tile(skew, (1, length))[:, : length * (width - 1)]
    rows = tiled.reshape(groups, length, width - 1)
    return rows[:, :, length - 1 : 3 * length - 1]


def hyena_core(extended, conv_weight, filters):
    length = filters.shape[1]
    values = extended.astype(jnp.float32)
    weights = conv_weight.astype(jnp.float32)
    shaped = (
        weights[:, 0, :] * values[2:]
        + weights[:, 1, :] * values[1:-1]
        + weights[:, 2, :] * values[:-2]
    )
    total = shaped.shape[0]
    out_rows = total - length
    query = shaped[length:, 0, :]
    mixed = (shaped[:, 1, :] * shaped[:, 2, :]).astype(jnp.bfloat16)
    group_count = filters.shape[0]
    channel_count = mixed.shape[1]
    blocks = mixed.reshape(total // length, length, group_count, channel_count // group_count)
    paired = jnp.concatenate([blocks[:-1], blocks[1:]], axis=1)
    table = lag_table(filters)
    filtered = jnp.einsum(
        "gts,bsgw->btgw", table, paired, preferred_element_type=jnp.float32
    )
    filtered = filtered.reshape(out_rows, channel_count)
    return (query * filtered).astype(jnp.bfloat16)


def local(tokens, norm_gain, in_weight, conv_weight, filters, out_weight):
    row_count = tokens.shape[0]
    chan_count = in_weight.shape[2]
    length = filters.shape[1]
    joined = jnp.concatenate([tokens, norm_gain[None, :]], axis=0)
    whole_joined = lax.all_gather(joined, "chan", axis=1, tiled=True)
    whole, gain_whole = whole_joined[:row_count], whole_joined[row_count]
    values = whole.astype(jnp.float32)
    mean_square = jnp.mean(values * values, axis=1, keepdims=True)
    normed = (values * lax.rsqrt(mean_square + 1e-06) * gain_whole.astype(jnp.float32)).astype(
        jnp.bfloat16
    )
    piece = lax.all_gather(in_weight, "seq", axis=0, tiled=True)
    panel = piece.reshape(piece.shape[0], 3 * chan_count)
    projected = jnp.dot(normed, panel, preferred_element_type=jnp.float32)
    streams = projected.astype(jnp.bfloat16).reshape(row_count, 3, chan_count)
    parts_count = lax.axis_size("seq")
    halo_rows = length + 2
    shift = [(i, i + 1) for i in range(parts_count - 1)]
    halo = lax.ppermute(streams[row_count - halo_rows :], "seq", shift)
    extended = jnp.concatenate([halo, streams], axis=0)
    gated = hyena_core(extended, conv_weight, filters)
    partial_out = jnp.dot(gated, out_weight, preferred_element_type=jnp.float32)
    summed = lax.psum_scatter(
        partial_out.astype(jnp.bfloat16), "chan", scatter_dimension=1, tiled=True
    )
    return (tokens.astype(jnp.float32) + summed.astype(jnp.float32)).astype(jnp.bfloat16)


def solution(mesh):
    return jax.shard_map(
        local,
        mesh=mesh,
        in_specs=(
            P("seq", "chan"),
            P("chan"),
            P("seq", None, "chan"),
            P(None, None, "chan"),
            P("chan", None),
            P("chan", None),
        ),
        out_specs=P("seq", "chan"),
        check_vma=False,
    )
```

```python
import functools

import jax
import jax.numpy as jnp
import numpy as np
from jax import lax
from jax.experimental import pallas as pl
from jax.experimental.pallas import tpu as pltpu
from jax.sharding import PartitionSpec as P

MESH = pl.DeviceIdType.MESH


def gather_kernel(parts, src_ref, out_ref, send_sem, recv_sem, local_sem):
    me = lax.axis_index("chan")
    row = lax.axis_index("seq")
    width = src_ref.shape[1]
    barrier = pltpu.get_barrier_semaphore()
    for k in range(1, parts):
        peer = lax.rem(me + k, parts)
        pl.semaphore_signal(barrier, inc=1, device_id=(row, peer), device_id_type=MESH)
    pl.semaphore_wait(barrier, parts - 1)
    mine = pl.ds(pl.multiple_of(me * width, width), width)
    local = pltpu.make_async_copy(src_ref, out_ref.at[:, mine], local_sem)
    local.start()
    copies = []
    for k in range(1, parts):
        peer = lax.rem(me + k, parts)
        copy = pltpu.make_async_remote_copy(
            src_ref=src_ref,
            dst_ref=out_ref.at[:, mine],
            send_sem=send_sem.at[k],
            recv_sem=recv_sem.at[k],
            device_id=(row, peer),
            device_id_type=MESH,
        )
        copy.start()
        copies.append(copy)
    local.wait()
    for copy in copies:
        copy.wait()


def gather_chan(block):
    parts = lax.axis_size("chan")
    rows, width = block.shape
    return pl.pallas_call(
        functools.partial(gather_kernel, parts),
        out_shape=jax.ShapeDtypeStruct((rows, parts * width), block.dtype),
        in_specs=[pl.BlockSpec(memory_space=pl.ANY)],
        out_specs=pl.BlockSpec(memory_space=pl.ANY),
        scratch_shapes=[
            pltpu.SemaphoreType.DMA((parts,)),
            pltpu.SemaphoreType.DMA((parts,)),
            pltpu.SemaphoreType.DMA(()),
        ],
        compiler_params=pltpu.CompilerParams(collective_id=0, has_side_effects=True),
        cost_estimate=pl.CostEstimate(
            flops=0, transcendentals=0, bytes_accessed=2 * rows * parts * width * 2
        ),
    )(block)


def lag_table(filters):
    groups, length = filters.shape
    width = 3 * length
    zeros = jnp.zeros((groups, length), filters.dtype)
    skew = jnp.concatenate([zeros, filters[:, ::-1], zeros], axis=1)
    tiled = jnp.tile(skew, (1, length))[:, : length * (width - 1)]
    rows = tiled.reshape(groups, length, width - 1)
    return rows[:, :, length - 1 : 3 * length - 1]


def hyena_core(extended, conv_weight, filters):
    length = filters.shape[1]
    values = extended.astype(jnp.float32)
    weights = conv_weight.astype(jnp.float32)
    shaped = (
        weights[:, 0, :] * values[2:]
        + weights[:, 1, :] * values[1:-1]
        + weights[:, 2, :] * values[:-2]
    )
    total = shaped.shape[0]
    out_rows = total - length
    query = shaped[length:, 0, :]
    mixed = (shaped[:, 1, :] * shaped[:, 2, :]).astype(jnp.bfloat16)
    group_count = filters.shape[0]
    channel_count = mixed.shape[1]
    blocks = mixed.reshape(total // length, length, group_count, channel_count // group_count)
    paired = jnp.concatenate([blocks[:-1], blocks[1:]], axis=1)
    table = lag_table(filters)
    filtered = jnp.einsum(
        "gts,bsgw->btgw", table, paired, preferred_element_type=jnp.float32
    )
    filtered = filtered.reshape(out_rows, channel_count)
    return (query * filtered).astype(jnp.bfloat16)


def local(tokens, norm_gain, in_weight, conv_weight, filters, out_weight):
    row_count = tokens.shape[0]
    chan_count = in_weight.shape[2]
    length = filters.shape[1]
    spare = jnp.zeros((15, tokens.shape[1]), tokens.dtype)
    joined = jnp.concatenate([tokens, norm_gain[None, :], spare], axis=0)
    whole_joined = gather_chan(joined)
    whole, gain_whole = whole_joined[:row_count], whole_joined[row_count]
    values = whole.astype(jnp.float32)
    mean_square = jnp.mean(values * values, axis=1, keepdims=True)
    normed = (values * lax.rsqrt(mean_square + 1e-06) * gain_whole.astype(jnp.float32)).astype(
        jnp.bfloat16
    )
    piece = lax.all_gather(in_weight, "seq", axis=0, tiled=True)
    panel = piece.reshape(piece.shape[0], 3 * chan_count)
    projected = jnp.dot(normed, panel, preferred_element_type=jnp.float32)
    streams = projected.astype(jnp.bfloat16).reshape(row_count, 3, chan_count)
    parts_count = lax.axis_size("seq")
    halo_rows = length + 2
    shift = [(i, i + 1) for i in range(parts_count - 1)]
    halo = lax.ppermute(streams[row_count - halo_rows :], "seq", shift)
    extended = jnp.concatenate([halo, streams], axis=0)
    gated = hyena_core(extended, conv_weight, filters)
    partial_out = jnp.dot(gated, out_weight, preferred_element_type=jnp.float32)
    summed = lax.psum_scatter(
        partial_out.astype(jnp.bfloat16), "chan", scatter_dimension=1, tiled=True
    )
    return (tokens.astype(jnp.float32) + summed.astype(jnp.float32)).astype(jnp.bfloat16)


def solution(mesh):
    return jax.shard_map(
        local,
        mesh=mesh,
        in_specs=(
            P("seq", "chan"),
            P("chan"),
            P("seq", None, "chan"),
            P(None, None, "chan"),
            P("chan", None),
            P("chan", None),
        ),
        out_specs=P("seq", "chan"),
        check_vma=False,
    )
```

```python
import jax
import jax.numpy as jnp
import numpy as np
from jax import lax
from jax.sharding import PartitionSpec as P


def lag_table(filters):
    groups, length = filters.shape
    width = 3 * length
    zeros = jnp.zeros((groups, length), filters.dtype)
    skew = jnp.concatenate([zeros, filters[:, ::-1], zeros], axis=1)
    tiled = jnp.tile(skew, (1, length))[:, : length * (width - 1)]
    rows = tiled.reshape(groups, length, width - 1)
    return rows[:, :, length - 1 : 3 * length - 1]


def hyena_core(extended, conv_weight, table):
    length = table.shape[1]
    values = extended.astype(jnp.float32)
    weights = conv_weight.astype(jnp.float32)
    shaped = (
        weights[:, 0, :] * values[2:]
        + weights[:, 1, :] * values[1:-1]
        + weights[:, 2, :] * values[:-2]
    )
    total = shaped.shape[0]
    out_rows = total - length
    query = shaped[length:, 0, :]
    mixed = (shaped[:, 1, :] * shaped[:, 2, :]).astype(jnp.bfloat16)
    group_count = table.shape[0]
    channel_count = mixed.shape[1]
    blocks = mixed.reshape(total // length, length, group_count, channel_count // group_count)
    paired = jnp.concatenate([blocks[:-1], blocks[1:]], axis=1)
    filtered = jnp.einsum(
        "gts,bsgw->btgw", table, paired, preferred_element_type=jnp.float32
    )
    filtered = filtered.reshape(out_rows, channel_count)
    return (query * filtered).astype(jnp.bfloat16)


def local(tokens, norm_gain, in_weight, conv_weight, filters, out_weight):
    row_count = tokens.shape[0]
    chan_count = in_weight.shape[2]
    length = filters.shape[1]
    joined = jnp.concatenate([tokens, norm_gain[None, :]], axis=0)
    whole_joined = lax.all_gather(joined, "chan", axis=1, tiled=True)
    table = lag_table(filters)
    table, whole_joined = lax.optimization_barrier((table, whole_joined))
    whole, gain_whole = whole_joined[:row_count], whole_joined[row_count]
    values = whole.astype(jnp.float32)
    mean_square = jnp.mean(values * values, axis=1, keepdims=True)
    normed = (values * lax.rsqrt(mean_square + 1e-06) * gain_whole.astype(jnp.float32)).astype(
        jnp.bfloat16
    )
    half = chan_count // 2
    projected = []
    for part in (in_weight[:, :, :half], in_weight[:, :, half:]):
        piece = lax.all_gather(part, "seq", axis=0, tiled=True)
        panel = piece.reshape(piece.shape[0], 3 * half)
        product = jnp.dot(normed, panel, preferred_element_type=jnp.float32)
        projected.append(product.astype(jnp.bfloat16).reshape(row_count, 3, half))
    streams = jnp.concatenate(projected, axis=2)
    parts_count = lax.axis_size("seq")
    halo_rows = length + 2
    shift = [(i, i + 1) for i in range(parts_count - 1)]
    halo = lax.ppermute(streams[row_count - halo_rows :], "seq", shift)
    extended = jnp.concatenate([halo, streams], axis=0)
    rows_half = row_count // 2
    results = []
    for start in (0, rows_half):
        window = extended[start : start + rows_half + halo_rows]
        gated = hyena_core(window, conv_weight, table)
        partial_out = jnp.dot(gated, out_weight, preferred_element_type=jnp.float32)
        summed = lax.psum_scatter(
            partial_out.astype(jnp.bfloat16), "chan", scatter_dimension=1, tiled=True
        )
        own = tokens[start : start + rows_half].astype(jnp.float32)
        results.append((own + summed.astype(jnp.float32)).astype(jnp.bfloat16))
    return jnp.concatenate(results, axis=0)


def solution(mesh):
    return jax.shard_map(
        local,
        mesh=mesh,
        in_specs=(
            P("seq", "chan"),
            P("chan"),
            P("seq", None, "chan"),
            P(None, None, "chan"),
            P("chan", None),
            P("chan", None),
        ),
        out_specs=P("seq", "chan"),
        check_vma=False,
    )
```

```python
import jax
import jax.numpy as jnp
import numpy as np
from jax import lax
from jax.sharding import Mesh, PartitionSpec as P


def lag_table(filters):
    groups, length = filters.shape
    width = 3 * length
    zeros = jnp.zeros((groups, length), filters.dtype)
    skew = jnp.concatenate([zeros, filters[:, ::-1], zeros], axis=1)
    tiled = jnp.tile(skew, (1, length))[:, : length * (width - 1)]
    rows = tiled.reshape(groups, length, width - 1)
    return rows[:, :, length - 1 : 3 * length - 1]


def hyena_core(extended, conv_weight, table):
    length = table.shape[1]
    values = extended.astype(jnp.float32)
    weights = conv_weight.astype(jnp.float32)
    shaped = (
        weights[:, 0, :] * values[2:]
        + weights[:, 1, :] * values[1:-1]
        + weights[:, 2, :] * values[:-2]
    )
    total = shaped.shape[0]
    out_rows = total - length
    query = shaped[length:, 0, :]
    mixed = (shaped[:, 1, :] * shaped[:, 2, :]).astype(jnp.bfloat16)
    group_count = table.shape[0]
    channel_count = mixed.shape[1]
    blocks = mixed.reshape(total // length, length, group_count, channel_count // group_count)
    paired = jnp.concatenate([blocks[:-1], blocks[1:]], axis=1)
    filtered = jnp.einsum(
        "gts,bsgw->btgw", table, paired, preferred_element_type=jnp.float32
    )
    filtered = filtered.reshape(out_rows, channel_count)
    return (query * filtered).astype(jnp.bfloat16)


def local(tokens, norm_gain, in_weight, conv_weight, filters, out_weight):
    row_count = tokens.shape[0]
    depth, _, chan_count = in_weight.shape
    length = filters.shape[1]
    joined = jnp.concatenate([tokens, norm_gain[None, :]], axis=0)
    whole_joined = lax.all_gather(joined, "chan", axis=1, tiled=True)
    table = lag_table(filters)
    table, whole_joined = lax.optimization_barrier((table, whole_joined))
    whole, gain_whole = whole_joined[:row_count], whole_joined[row_count]
    values = whole.astype(jnp.float32)
    mean_square = jnp.mean(values * values, axis=1, keepdims=True)
    normed = (values * lax.rsqrt(mean_square + 1e-06) * gain_whole.astype(jnp.float32)).astype(
        jnp.bfloat16
    )
    x_count = lax.axis_size("x")
    x_me = lax.axis_index("x")
    core_me = lax.axis_index("core")
    own = [in_weight]
    for k in range(1, x_count):
        own.append(lax.ppermute(in_weight, "x", [(i, (i + k) % x_count) for i in range(x_count)]))
    mine = jnp.stack(own)
    other = lax.ppermute(mine, "core", [(0, 1), (1, 0)])
    projected = None
    for parity, blocks in ((core_me, mine), (1 - core_me, other)):
        for k in range(x_count):
            owner = 2 * lax.rem(x_me - k + x_count, x_count) + parity
            rows = lax.dynamic_slice_in_dim(normed, owner * depth, depth, axis=1)
            panel = blocks[k].reshape(depth, 3 * chan_count)
            term = jnp.dot(rows, panel, preferred_element_type=jnp.float32)
            projected = term if projected is None else projected + term
    streams = projected.astype(jnp.bfloat16).reshape(row_count, 3, chan_count)
    parts_count = lax.axis_size(SEQ)
    halo_rows = length + 2
    shift = [(i, i + 1) for i in range(parts_count - 1)]
    halo = lax.ppermute(streams[row_count - halo_rows :], SEQ, shift)
    extended = jnp.concatenate([halo, streams], axis=0)
    gated = hyena_core(extended, conv_weight, table)
    partial_out = jnp.dot(gated, out_weight, preferred_element_type=jnp.float32)
    summed = lax.psum_scatter(
        partial_out.astype(jnp.bfloat16), "chan", scatter_dimension=1, tiled=True
    )
    return (tokens.astype(jnp.float32) + summed.astype(jnp.float32)).astype(jnp.bfloat16)


SEQ = ("x", "core")


def solution(mesh):
    seq_count, chan_count = mesh.devices.shape
    split = Mesh(mesh.devices.reshape(seq_count // 2, 2, chan_count), ("x", "core", "chan"))
    return jax.shard_map(
        local,
        mesh=split,
        in_specs=(
            P(SEQ, "chan"),
            P("chan"),
            P(SEQ, None, "chan"),
            P(None, None, "chan"),
            P("chan", None),
            P("chan", None),
        ),
        out_specs=P(SEQ, "chan"),
        check_vma=False,
    )
```

```python
import jax
import jax.numpy as jnp
import numpy as np
from jax import lax
from jax.sharding import Mesh, PartitionSpec as P


def lag_table(filters):
    groups, length = filters.shape
    width = 3 * length
    zeros = jnp.zeros((groups, length), filters.dtype)
    skew = jnp.concatenate([zeros, filters[:, ::-1], zeros], axis=1)
    tiled = jnp.tile(skew, (1, length))[:, : length * (width - 1)]
    rows = tiled.reshape(groups, length, width - 1)
    return rows[:, :, length - 1 : 3 * length - 1]


def hyena_core(extended, conv_weight, table):
    length = table.shape[1]
    values = extended.astype(jnp.float32)
    weights = conv_weight.astype(jnp.float32)
    shaped = (
        weights[:, 0, :] * values[2:]
        + weights[:, 1, :] * values[1:-1]
        + weights[:, 2, :] * values[:-2]
    )
    total = shaped.shape[0]
    out_rows = total - length
    query = shaped[length:, 0, :]
    mixed = (shaped[:, 1, :] * shaped[:, 2, :]).astype(jnp.bfloat16)
    group_count = table.shape[0]
    channel_count = mixed.shape[1]
    blocks = mixed.reshape(total // length, length, group_count, channel_count // group_count)
    paired = jnp.concatenate([blocks[:-1], blocks[1:]], axis=1)
    filtered = jnp.einsum(
        "gts,bsgw->btgw", table, paired, preferred_element_type=jnp.float32
    )
    filtered = filtered.reshape(out_rows, channel_count)
    return (query * filtered).astype(jnp.bfloat16)


def local(tokens, norm_gain, in_weight, conv_weight, filters, out_weight):
    row_count = tokens.shape[0]
    depth, _, chan_count = in_weight.shape
    length = filters.shape[1]
    joined = jnp.concatenate([tokens, norm_gain[None, :]], axis=0)
    whole_joined = lax.all_gather(joined, "chan", axis=1, tiled=True)
    table = lag_table(filters)
    table, whole_joined = lax.optimization_barrier((table, whole_joined))
    whole, gain_whole = whole_joined[:row_count], whole_joined[row_count]
    values = whole.astype(jnp.float32)
    mean_square = jnp.mean(values * values, axis=1, keepdims=True)
    normed = (values * lax.rsqrt(mean_square + 1e-06) * gain_whole.astype(jnp.float32)).astype(
        jnp.bfloat16
    )
    quarter = chan_count // 4
    rest = chan_count - quarter
    direct = in_weight[:, :, :quarter]
    direct, whole_joined = lax.optimization_barrier((direct, whole_joined))
    direct_whole = lax.all_gather(direct, SEQ, axis=0, tiled=True)
    moved = in_weight[:, :, quarter:]
    x_count = lax.axis_size("x")
    x_me = lax.axis_index("x")
    core_me = lax.axis_index("core")
    own = [moved]
    for k in range(1, x_count):
        own.append(lax.ppermute(moved, "x", [(i, (i + k) % x_count) for i in range(x_count)]))
    mine = jnp.stack(own)
    other = lax.ppermute(mine, "core", [(0, 1), (1, 0)])
    by_owner = normed.reshape(row_count, x_count, 2, depth)
    projected_rest = None
    for parity, blocks in ((core_me, mine), (1 - core_me, other)):
        chosen = lax.dynamic_index_in_dim(by_owner, parity, axis=2, keepdims=False)
        ordered = jnp.roll(chosen[:, ::-1], x_me + 1, axis=1)
        term = jnp.dot(
            ordered.reshape(row_count, x_count * depth),
            blocks.reshape(x_count * depth, 3 * rest),
            preferred_element_type=jnp.float32,
        )
        projected_rest = term if projected_rest is None else projected_rest + term
    projected_direct = jnp.dot(
        normed,
        direct_whole.reshape(direct_whole.shape[0], 3 * quarter),
        preferred_element_type=jnp.float32,
    )
    streams = jnp.concatenate(
        [
            projected_direct.astype(jnp.bfloat16).reshape(row_count, 3, quarter),
            projected_rest.astype(jnp.bfloat16).reshape(row_count, 3, rest),
        ],
        axis=2,
    )
    parts_count = lax.axis_size(SEQ)
    halo_rows = length + 2
    shift = [(i, i + 1) for i in range(parts_count - 1)]
    halo = lax.ppermute(streams[row_count - halo_rows :], SEQ, shift)
    extended = jnp.concatenate([halo, streams], axis=0)
    gated = hyena_core(extended, conv_weight, table)
    partial_out = jnp.dot(gated, out_weight, preferred_element_type=jnp.float32)
    summed = lax.psum_scatter(
        partial_out.astype(jnp.bfloat16), "chan", scatter_dimension=1, tiled=True
    )
    return (tokens.astype(jnp.float32) + summed.astype(jnp.float32)).astype(jnp.bfloat16)


SEQ = ("x", "core")


def solution(mesh):
    seq_count, chan_count = mesh.devices.shape
    split = Mesh(mesh.devices.reshape(seq_count // 2, 2, chan_count), ("x", "core", "chan"))
    return jax.shard_map(
        local,
        mesh=split,
        in_specs=(
            P(SEQ, "chan"),
            P("chan"),
            P(SEQ, None, "chan"),
            P(None, None, "chan"),
            P("chan", None),
            P("chan", None),
        ),
        out_specs=P(SEQ, "chan"),
        check_vma=False,
    )
```

```python
import jax
import jax.numpy as jnp
import numpy as np
from jax import lax
from jax.sharding import Mesh, PartitionSpec as P


def lag_table(filters):
    groups, length = filters.shape
    width = 3 * length
    zeros = jnp.zeros((groups, length), filters.dtype)
    skew = jnp.concatenate([zeros, filters[:, ::-1], zeros], axis=1)
    tiled = jnp.tile(skew, (1, length))[:, : length * (width - 1)]
    rows = tiled.reshape(groups, length, width - 1)
    return rows[:, :, length - 1 : 3 * length - 1]


def hyena_core(extended, conv_weight, table):
    length = table.shape[1]
    values = extended.astype(jnp.float32)
    weights = conv_weight.astype(jnp.float32)
    shaped = (
        weights[:, 0, :] * values[2:]
        + weights[:, 1, :] * values[1:-1]
        + weights[:, 2, :] * values[:-2]
    )
    total = shaped.shape[0]
    out_rows = total - length
    query = shaped[length:, 0, :]
    mixed = (shaped[:, 1, :] * shaped[:, 2, :]).astype(jnp.bfloat16)
    group_count = table.shape[0]
    channel_count = mixed.shape[1]
    blocks = mixed.reshape(total // length, length, group_count, channel_count // group_count)
    paired = jnp.concatenate([blocks[:-1], blocks[1:]], axis=1)
    filtered = jnp.einsum(
        "gts,bsgw->btgw", table, paired, preferred_element_type=jnp.float32
    )
    filtered = filtered.reshape(out_rows, channel_count)
    return (query * filtered).astype(jnp.bfloat16)


def local(tokens, norm_gain, in_weight, conv_weight, filters, out_weight):
    row_count = tokens.shape[0]
    depth, _, chan_count = in_weight.shape
    length = filters.shape[1]
    joined = jnp.concatenate([tokens, norm_gain[None, :]], axis=0)
    whole_joined = lax.all_gather(joined, "chan", axis=1, tiled=True)
    table = lag_table(filters)
    table, whole_joined = lax.optimization_barrier((table, whole_joined))
    whole, gain_whole = whole_joined[:row_count], whole_joined[row_count]
    values = whole.astype(jnp.float32)
    mean_square = jnp.mean(values * values, axis=1, keepdims=True)
    normed = (values * lax.rsqrt(mean_square + 1e-06) * gain_whole.astype(jnp.float32)).astype(
        jnp.bfloat16
    )
    x_count = lax.axis_size("x")
    x_me = lax.axis_index("x")
    core_me = lax.axis_index("core")
    own = [in_weight]
    for k in range(1, x_count):
        own.append(lax.ppermute(in_weight, "x", [(i, (i + k) % x_count) for i in range(x_count)]))
    mine = jnp.stack(own)
    other = lax.ppermute(mine, "core", [(0, 1), (1, 0)])
    projected = None
    for parity, blocks in ((core_me, mine), (1 - core_me, other)):
        pieces = []
        for k in range(x_count):
            owner = 2 * lax.rem(x_me - k + x_count, x_count) + parity
            pieces.append(lax.dynamic_slice_in_dim(normed, owner * depth, depth, axis=1))
        rows = jnp.concatenate(pieces, axis=1)
        panel = blocks.reshape(x_count * depth, 3 * chan_count)
        term = jnp.dot(rows, panel, preferred_element_type=jnp.float32)
        projected = term if projected is None else projected + term
    streams = projected.astype(jnp.bfloat16).reshape(row_count, 3, chan_count)
    parts_count = lax.axis_size(SEQ)
    halo_rows = length + 2
    shift = [(i, i + 1) for i in range(parts_count - 1)]
    halo = lax.ppermute(streams[row_count - halo_rows :], SEQ, shift)
    extended = jnp.concatenate([halo, streams], axis=0)
    gated = hyena_core(extended, conv_weight, table)
    partial_out = jnp.dot(gated, out_weight, preferred_element_type=jnp.float32)
    summed = lax.psum_scatter(
        partial_out.astype(jnp.bfloat16), "chan", scatter_dimension=1, tiled=True
    )
    return (tokens.astype(jnp.float32) + summed.astype(jnp.float32)).astype(jnp.bfloat16)


SEQ = ("x", "core")


def solution(mesh):
    seq_count, chan_count = mesh.devices.shape
    split = Mesh(mesh.devices.reshape(seq_count // 2, 2, chan_count), ("x", "core", "chan"))
    return jax.shard_map(
        local,
        mesh=split,
        in_specs=(
            P(SEQ, "chan"),
            P("chan"),
            P(SEQ, None, "chan"),
            P(None, None, "chan"),
            P("chan", None),
            P("chan", None),
        ),
        out_specs=P(SEQ, "chan"),
        check_vma=False,
    )
```

```python
import jax
import jax.numpy as jnp
import numpy as np
from jax import lax
from jax.sharding import Mesh, PartitionSpec as P


def lag_table(filters):
    groups, length = filters.shape
    width = 3 * length
    zeros = jnp.zeros((groups, length), filters.dtype)
    skew = jnp.concatenate([zeros, filters[:, ::-1], zeros], axis=1)
    tiled = jnp.tile(skew, (1, length))[:, : length * (width - 1)]
    rows = tiled.reshape(groups, length, width - 1)
    return rows[:, :, length - 1 : 3 * length - 1]


def hyena_core(extended, conv_weight, table):
    length = table.shape[1]
    values = extended.astype(jnp.float32)
    weights = conv_weight.astype(jnp.float32)
    shaped = (
        weights[:, 0, :] * values[2:]
        + weights[:, 1, :] * values[1:-1]
        + weights[:, 2, :] * values[:-2]
    )
    total = shaped.shape[0]
    out_rows = total - length
    query = shaped[length:, 0, :]
    mixed = (shaped[:, 1, :] * shaped[:, 2, :]).astype(jnp.bfloat16)
    group_count = table.shape[0]
    channel_count = mixed.shape[1]
    blocks = mixed.reshape(total // length, length, group_count, channel_count // group_count)
    paired = jnp.concatenate([blocks[:-1], blocks[1:]], axis=1)
    filtered = jnp.einsum(
        "gts,bsgw->btgw", table, paired, preferred_element_type=jnp.float32
    )
    filtered = filtered.reshape(out_rows, channel_count)
    return (query * filtered).astype(jnp.bfloat16)


def local(tokens, norm_gain, in_weight, conv_weight, filters, out_weight):
    row_count = tokens.shape[0]
    depth, _, chan_count = in_weight.shape
    length = filters.shape[1]
    joined = jnp.concatenate([tokens, norm_gain[None, :]], axis=0)
    whole_joined = lax.all_gather(joined, "chan", axis=1, tiled=True)
    table = lag_table(filters)
    table, whole_joined = lax.optimization_barrier((table, whole_joined))
    whole, gain_whole = whole_joined[:row_count], whole_joined[row_count]
    values = whole.astype(jnp.float32)
    mean_square = jnp.mean(values * values, axis=1, keepdims=True)
    normed = (values * lax.rsqrt(mean_square + 1e-06) * gain_whole.astype(jnp.float32)).astype(
        jnp.bfloat16
    )
    x_count = lax.axis_size("x")
    x_me = lax.axis_index("x")
    core_me = lax.axis_index("core")
    own = [in_weight]
    for k in range(1, x_count):
        own.append(lax.ppermute(in_weight, "x", [(i, (i + k) % x_count) for i in range(x_count)]))
    mine = jnp.concatenate([block.transpose(1, 0, 2) for block in own], axis=1)
    other = lax.ppermute(mine, "core", [(0, 1), (1, 0)])
    projected = None
    for parity, blocks in ((core_me, mine), (1 - core_me, other)):
        pieces = []
        for k in range(x_count):
            owner = 2 * lax.rem(x_me - k + x_count, x_count) + parity
            pieces.append(lax.dynamic_slice_in_dim(normed, owner * depth, depth, axis=1))
        rows = jnp.concatenate(pieces, axis=1)
        term = jnp.einsum("rk,ikc->ric", rows, blocks, preferred_element_type=jnp.float32)
        projected = term if projected is None else projected + term
    streams = projected.astype(jnp.bfloat16)
    parts_count = lax.axis_size(SEQ)
    halo_rows = length + 2
    shift = [(i, i + 1) for i in range(parts_count - 1)]
    halo = lax.ppermute(streams[row_count - halo_rows :], SEQ, shift)
    extended = jnp.concatenate([halo, streams], axis=0)
    gated = hyena_core(extended, conv_weight, table)
    partial_out = jnp.dot(gated, out_weight, preferred_element_type=jnp.float32)
    summed = lax.psum_scatter(
        partial_out.astype(jnp.bfloat16), "chan", scatter_dimension=1, tiled=True
    )
    return (tokens.astype(jnp.float32) + summed.astype(jnp.float32)).astype(jnp.bfloat16)


SEQ = ("x", "core")


def solution(mesh):
    seq_count, chan_count = mesh.devices.shape
    split = Mesh(mesh.devices.reshape(seq_count // 2, 2, chan_count), ("x", "core", "chan"))
    return jax.shard_map(
        local,
        mesh=split,
        in_specs=(
            P(SEQ, "chan"),
            P("chan"),
            P(SEQ, None, "chan"),
            P(None, None, "chan"),
            P("chan", None),
            P("chan", None),
        ),
        out_specs=P(SEQ, "chan"),
        check_vma=False,
    )
```

```python
import jax
import jax.numpy as jnp
import numpy as np
from jax import lax
from jax.sharding import Mesh, PartitionSpec as P


def lag_table(filters):
    groups, length = filters.shape
    width = 3 * length
    zeros = jnp.zeros((groups, length), filters.dtype)
    skew = jnp.concatenate([zeros, filters[:, ::-1], zeros], axis=1)
    tiled = jnp.tile(skew, (1, length))[:, : length * (width - 1)]
    rows = tiled.reshape(groups, length, width - 1)
    return rows[:, :, length - 1 : 3 * length - 1]


def hyena_core(extended, conv_weight, table):
    length = table.shape[1]
    values = extended.astype(jnp.float32)
    weights = conv_weight.astype(jnp.float32)
    shaped = (
        weights[:, 0, :] * values[2:]
        + weights[:, 1, :] * values[1:-1]
        + weights[:, 2, :] * values[:-2]
    )
    total = shaped.shape[0]
    out_rows = total - length
    query = shaped[length:, 0, :]
    mixed = (shaped[:, 1, :] * shaped[:, 2, :]).astype(jnp.bfloat16)
    group_count = table.shape[0]
    channel_count = mixed.shape[1]
    blocks = mixed.reshape(total // length, length, group_count, channel_count // group_count)
    paired = jnp.concatenate([blocks[:-1], blocks[1:]], axis=1)
    filtered = jnp.einsum(
        "gts,bsgw->btgw", table, paired, preferred_element_type=jnp.float32
    )
    filtered = filtered.reshape(out_rows, channel_count)
    return (query * filtered).astype(jnp.bfloat16)


def local(tokens, norm_gain, in_weight, conv_weight, filters, out_weight):
    row_count = tokens.shape[0]
    depth, _, chan_count = in_weight.shape
    length = filters.shape[1]
    joined = jnp.concatenate([tokens, norm_gain[None, :]], axis=0)
    whole_joined = lax.all_gather(joined, "chan", axis=1, tiled=True)
    table = lag_table(filters)
    table, whole_joined = lax.optimization_barrier((table, whole_joined))
    whole, gain_whole = whole_joined[:row_count], whole_joined[row_count]
    values = whole.astype(jnp.float32)
    mean_square = jnp.mean(values * values, axis=1, keepdims=True)
    normed = (values * lax.rsqrt(mean_square + 1e-06) * gain_whole.astype(jnp.float32)).astype(
        jnp.bfloat16
    )
    x_count = lax.axis_size("x")
    x_me = lax.axis_index("x")
    core_me = lax.axis_index("core")
    own = [in_weight]
    for k in range(1, x_count):
        own.append(lax.ppermute(in_weight, "x", [(i, (i + k) % x_count) for i in range(x_count)]))
    swap = [(0, 1), (1, 0)]
    forwarded = [lax.ppermute(block, "core", swap) for block in own]
    own, normed, table = lax.optimization_barrier((tuple(own), normed, table))
    mine = jnp.concatenate([block.transpose(1, 0, 2) for block in own], axis=1)
    other = jnp.concatenate([block.transpose(1, 0, 2) for block in forwarded], axis=1)
    projected = None
    for parity, blocks in ((core_me, mine), (1 - core_me, other)):
        pieces = []
        for k in range(x_count):
            owner = 2 * lax.rem(x_me - k + x_count, x_count) + parity
            pieces.append(lax.dynamic_slice_in_dim(normed, owner * depth, depth, axis=1))
        rows = jnp.concatenate(pieces, axis=1)
        term = jnp.einsum("rk,ikc->ric", rows, blocks, preferred_element_type=jnp.float32)
        projected = term if projected is None else projected + term
    streams = projected.astype(jnp.bfloat16)
    parts_count = lax.axis_size(SEQ)
    halo_rows = length + 2
    shift = [(i, i + 1) for i in range(parts_count - 1)]
    halo = lax.ppermute(streams[row_count - halo_rows :], SEQ, shift)
    extended = jnp.concatenate([halo, streams], axis=0)
    gated = hyena_core(extended, conv_weight, table)
    partial_out = jnp.dot(gated, out_weight, preferred_element_type=jnp.float32)
    summed = lax.psum_scatter(
        partial_out.astype(jnp.bfloat16), "chan", scatter_dimension=1, tiled=True
    )
    return (tokens.astype(jnp.float32) + summed.astype(jnp.float32)).astype(jnp.bfloat16)


SEQ = ("x", "core")


def solution(mesh):
    seq_count, chan_count = mesh.devices.shape
    split = Mesh(mesh.devices.reshape(seq_count // 2, 2, chan_count), ("x", "core", "chan"))
    return jax.shard_map(
        local,
        mesh=split,
        in_specs=(
            P(SEQ, "chan"),
            P("chan"),
            P(SEQ, None, "chan"),
            P(None, None, "chan"),
            P("chan", None),
            P("chan", None),
        ),
        out_specs=P(SEQ, "chan"),
        check_vma=False,
    )
```

```python
import jax
import jax.numpy as jnp
import numpy as np
from jax import lax
from jax.sharding import Mesh, PartitionSpec as P


def lag_table(filters):
    groups, length = filters.shape
    width = 3 * length
    zeros = jnp.zeros((groups, length), filters.dtype)
    skew = jnp.concatenate([zeros, filters[:, ::-1], zeros], axis=1)
    tiled = jnp.tile(skew, (1, length))[:, : length * (width - 1)]
    rows = tiled.reshape(groups, length, width - 1)
    return rows[:, :, length - 1 : 3 * length - 1]


def hyena_core(extended, conv_weight, table):
    length = table.shape[1]
    values = extended.astype(jnp.float32)
    weights = conv_weight.astype(jnp.float32)
    shaped = (
        weights[:, 0, :] * values[2:]
        + weights[:, 1, :] * values[1:-1]
        + weights[:, 2, :] * values[:-2]
    )
    total = shaped.shape[0]
    out_rows = total - length
    query = shaped[length:, 0, :]
    mixed = (shaped[:, 1, :] * shaped[:, 2, :]).astype(jnp.bfloat16)
    group_count = table.shape[0]
    channel_count = mixed.shape[1]
    blocks = mixed.reshape(total // length, length, group_count, channel_count // group_count)
    paired = jnp.concatenate([blocks[:-1], blocks[1:]], axis=1)
    filtered = jnp.einsum(
        "gts,bsgw->btgw", table, paired, preferred_element_type=jnp.float32
    )
    filtered = filtered.reshape(out_rows, channel_count)
    return (query * filtered).astype(jnp.bfloat16)


def local(tokens, norm_gain, in_weight, conv_weight, filters, out_weight):
    row_count = tokens.shape[0]
    depth, _, chan_count = in_weight.shape
    length = filters.shape[1]
    joined = jnp.concatenate([tokens, norm_gain[None, :]], axis=0)
    whole_joined = lax.all_gather(joined, "chan", axis=1, tiled=True)
    table = lag_table(filters)
    table, whole_joined = lax.optimization_barrier((table, whole_joined))
    whole, gain_whole = whole_joined[:row_count], whole_joined[row_count]
    values = whole.astype(jnp.float32)
    mean_square = jnp.mean(values * values, axis=1, keepdims=True)
    normed = (values * lax.rsqrt(mean_square + 1e-06) * gain_whole.astype(jnp.float32)).astype(
        jnp.bfloat16
    )
    x_count = lax.axis_size("x")
    x_me = lax.axis_index("x")
    core_me = lax.axis_index("core")
    own = [in_weight]
    for k in range(1, x_count):
        own.append(lax.ppermute(in_weight, "x", [(i, (i + k) % x_count) for i in range(x_count)]))
    swap = [(0, 1), (1, 0)]
    forwarded = [lax.ppermute(own[0], "core", swap)]
    for block in own[1:]:
        block, normed = lax.optimization_barrier((block, normed))
        forwarded.append(lax.ppermute(block, "core", swap))
    own, normed, table = lax.optimization_barrier((tuple(own), normed, table))
    mine = jnp.concatenate([block.transpose(1, 0, 2) for block in own], axis=1)
    other = jnp.concatenate([block.transpose(1, 0, 2) for block in forwarded], axis=1)
    projected = None
    for parity, blocks in ((core_me, mine), (1 - core_me, other)):
        pieces = []
        for k in range(x_count):
            owner = 2 * lax.rem(x_me - k + x_count, x_count) + parity
            pieces.append(lax.dynamic_slice_in_dim(normed, owner * depth, depth, axis=1))
        rows = jnp.concatenate(pieces, axis=1)
        term = jnp.einsum("rk,ikc->ric", rows, blocks, preferred_element_type=jnp.float32)
        projected = term if projected is None else projected + term
    streams = projected.astype(jnp.bfloat16)
    parts_count = lax.axis_size(SEQ)
    halo_rows = length + 2
    shift = [(i, i + 1) for i in range(parts_count - 1)]
    halo = lax.ppermute(streams[row_count - halo_rows :], SEQ, shift)
    extended = jnp.concatenate([halo, streams], axis=0)
    gated = hyena_core(extended, conv_weight, table)
    partial_out = jnp.dot(gated, out_weight, preferred_element_type=jnp.float32)
    summed = lax.psum_scatter(
        partial_out.astype(jnp.bfloat16), "chan", scatter_dimension=1, tiled=True
    )
    return (tokens.astype(jnp.float32) + summed.astype(jnp.float32)).astype(jnp.bfloat16)


SEQ = ("x", "core")


def solution(mesh):
    seq_count, chan_count = mesh.devices.shape
    split = Mesh(mesh.devices.reshape(seq_count // 2, 2, chan_count), ("x", "core", "chan"))
    return jax.shard_map(
        local,
        mesh=split,
        in_specs=(
            P(SEQ, "chan"),
            P("chan"),
            P(SEQ, None, "chan"),
            P(None, None, "chan"),
            P("chan", None),
            P("chan", None),
        ),
        out_specs=P(SEQ, "chan"),
        check_vma=False,
    )
```

```python
import jax
import jax.numpy as jnp
import numpy as np
from jax import lax
from jax.sharding import Mesh, PartitionSpec as P


def lag_table(filters):
    groups, length = filters.shape
    width = 3 * length
    zeros = jnp.zeros((groups, length), filters.dtype)
    skew = jnp.concatenate([zeros, filters[:, ::-1], zeros], axis=1)
    tiled = jnp.tile(skew, (1, length))[:, : length * (width - 1)]
    rows = tiled.reshape(groups, length, width - 1)
    return rows[:, :, length - 1 : 3 * length - 1]


def hyena_core(extended, conv_weight, table):
    length = table.shape[1]
    values = extended.astype(jnp.float32)
    weights = conv_weight.astype(jnp.float32)
    shaped = (
        weights[:, 0, :] * values[2:]
        + weights[:, 1, :] * values[1:-1]
        + weights[:, 2, :] * values[:-2]
    )
    total = shaped.shape[0]
    out_rows = total - length
    query = shaped[length:, 0, :]
    mixed = (shaped[:, 1, :] * shaped[:, 2, :]).astype(jnp.bfloat16)
    group_count = table.shape[0]
    channel_count = mixed.shape[1]
    blocks = mixed.reshape(total // length, length, group_count, channel_count // group_count)
    paired = jnp.concatenate([blocks[:-1], blocks[1:]], axis=1)
    filtered = jnp.einsum(
        "gts,bsgw->btgw", table, paired, preferred_element_type=jnp.float32
    )
    filtered = filtered.reshape(out_rows, channel_count)
    return (query * filtered).astype(jnp.bfloat16)


def local(tokens, norm_gain, in_weight, conv_weight, filters, out_weight):
    row_count = tokens.shape[0]
    depth, _, chan_count = in_weight.shape
    length = filters.shape[1]
    joined = jnp.concatenate([tokens, norm_gain[None, :]], axis=0)
    whole_joined = lax.all_gather(joined, "chan", axis=1, tiled=True)
    table = lag_table(filters)
    table, whole_joined = lax.optimization_barrier((table, whole_joined))
    whole, gain_whole = whole_joined[:row_count], whole_joined[row_count]
    values = whole.astype(jnp.float32)
    mean_square = jnp.mean(values * values, axis=1, keepdims=True)
    normed = (values * lax.rsqrt(mean_square + 1e-06) * gain_whole.astype(jnp.float32)).astype(
        jnp.bfloat16
    )
    x_count = lax.axis_size("x")
    x_me = lax.axis_index("x")
    core_me = lax.axis_index("core")
    own = [in_weight]
    for k in range(1, x_count):
        own.append(lax.ppermute(in_weight, "x", [(i, (i + k) % x_count) for i in range(x_count)]))
    ordered = []
    for parity in (core_me, 1 - core_me):
        pieces = []
        for k in range(x_count):
            owner = 2 * lax.rem(x_me - k + x_count, x_count) + parity
            pieces.append(lax.dynamic_slice_in_dim(normed, owner * depth, depth, axis=1))
        ordered.append(jnp.concatenate(pieces, axis=1))
    ordered = tuple(ordered)
    swap = [(0, 1), (1, 0)]
    forwarded = [lax.ppermute(own[0], "core", swap)]
    for block in own[1:]:
        block, ordered = lax.optimization_barrier((block, ordered))
        forwarded.append(lax.ppermute(block, "core", swap))
    own, ordered, table = lax.optimization_barrier((tuple(own), ordered, table))
    mine = jnp.concatenate([block.transpose(1, 0, 2) for block in own], axis=1)
    other = jnp.concatenate([block.transpose(1, 0, 2) for block in forwarded], axis=1)
    projected = None
    for rows, blocks in zip(ordered, (mine, other)):
        term = jnp.einsum("rk,ikc->ric", rows, blocks, preferred_element_type=jnp.float32)
        projected = term if projected is None else projected + term
    streams = projected.astype(jnp.bfloat16)
    parts_count = lax.axis_size(SEQ)
    halo_rows = length + 2
    shift = [(i, i + 1) for i in range(parts_count - 1)]
    halo = lax.ppermute(streams[row_count - halo_rows :], SEQ, shift)
    extended = jnp.concatenate([halo, streams], axis=0)
    gated = hyena_core(extended, conv_weight, table)
    partial_out = jnp.dot(gated, out_weight, preferred_element_type=jnp.float32)
    summed = lax.psum_scatter(
        partial_out.astype(jnp.bfloat16), "chan", scatter_dimension=1, tiled=True
    )
    return (tokens.astype(jnp.float32) + summed.astype(jnp.float32)).astype(jnp.bfloat16)


SEQ = ("x", "core")


def solution(mesh):
    seq_count, chan_count = mesh.devices.shape
    split = Mesh(mesh.devices.reshape(seq_count // 2, 2, chan_count), ("x", "core", "chan"))
    return jax.shard_map(
        local,
        mesh=split,
        in_specs=(
            P(SEQ, "chan"),
            P("chan"),
            P(SEQ, None, "chan"),
            P(None, None, "chan"),
            P("chan", None),
            P("chan", None),
        ),
        out_specs=P(SEQ, "chan"),
        check_vma=False,
    )
```

```python
import jax
import jax.numpy as jnp
import numpy as np
from jax import lax
from jax.sharding import Mesh, PartitionSpec as P


def lag_table(filters):
    groups, length = filters.shape
    width = 3 * length
    zeros = jnp.zeros((groups, length), filters.dtype)
    skew = jnp.concatenate([zeros, filters[:, ::-1], zeros], axis=1)
    tiled = jnp.tile(skew, (1, length))[:, : length * (width - 1)]
    rows = tiled.reshape(groups, length, width - 1)
    return rows[:, :, length - 1 : 3 * length - 1]


def hyena_core(extended, conv_weight, table):
    length = table.shape[1]
    values = extended.astype(jnp.float32)
    weights = conv_weight.astype(jnp.float32)
    shaped = (
        weights[:, 0, :] * values[2:]
        + weights[:, 1, :] * values[1:-1]
        + weights[:, 2, :] * values[:-2]
    )
    total = shaped.shape[0]
    out_rows = total - length
    query = shaped[length:, 0, :]
    mixed = (shaped[:, 1, :] * shaped[:, 2, :]).astype(jnp.bfloat16)
    group_count = table.shape[0]
    channel_count = mixed.shape[1]
    blocks = mixed.reshape(total // length, length, group_count, channel_count // group_count)
    paired = jnp.concatenate([blocks[:-1], blocks[1:]], axis=1)
    filtered = jnp.einsum(
        "gts,bsgw->btgw", table, paired, preferred_element_type=jnp.float32
    )
    filtered = filtered.reshape(out_rows, channel_count)
    return (query * filtered).astype(jnp.bfloat16)


def local(tokens, norm_gain, in_weight, conv_weight, filters, out_weight):
    row_count = tokens.shape[0]
    depth, _, chan_count = in_weight.shape
    length = filters.shape[1]
    joined = jnp.concatenate([tokens, norm_gain[None, :]], axis=0)
    whole_joined = lax.all_gather(joined, "chan", axis=1, tiled=True)
    table = lag_table(filters)
    table, whole_joined = lax.optimization_barrier((table, whole_joined))
    whole, gain_whole = whole_joined[:row_count], whole_joined[row_count]
    values = whole.astype(jnp.float32)
    mean_square = jnp.mean(values * values, axis=1, keepdims=True)
    normed = (values * lax.rsqrt(mean_square + 1e-06) * gain_whole.astype(jnp.float32)).astype(
        jnp.bfloat16
    )
    x_count = lax.axis_size("x")
    x_me = lax.axis_index("x")
    core_me = lax.axis_index("core")
    own = [in_weight]
    for k in range(1, x_count):
        own.append(lax.ppermute(in_weight, "x", [(i, (i + k) % x_count) for i in range(x_count)]))
    ordered = []
    for parity in (core_me, 1 - core_me):
        pieces = []
        for k in range(x_count):
            owner = 2 * lax.rem(x_me - k + x_count, x_count) + parity
            pieces.append(lax.dynamic_slice_in_dim(normed, owner * depth, depth, axis=1))
        ordered.append(jnp.concatenate(pieces, axis=1))
    ordered = tuple(ordered)
    swap = [(0, 1), (1, 0)]
    forwarded = [lax.ppermute(own[0], "core", swap)]
    for block in own[1:]:
        block, ordered = lax.optimization_barrier((block, ordered))
        forwarded.append(lax.ppermute(block, "core", swap))
    own, ordered, table = lax.optimization_barrier((tuple(own), ordered, table))
    mine = jnp.concatenate([block.transpose(1, 0, 2) for block in own], axis=1)
    projected = jnp.einsum("rk,ikc->ric", ordered[0], mine, preferred_element_type=jnp.float32)
    projected, forwarded = lax.optimization_barrier((projected, tuple(forwarded)))
    other = jnp.concatenate([block.transpose(1, 0, 2) for block in forwarded], axis=1)
    projected = projected + jnp.einsum(
        "rk,ikc->ric", ordered[1], other, preferred_element_type=jnp.float32
    )
    streams = projected.astype(jnp.bfloat16)
    parts_count = lax.axis_size(SEQ)
    halo_rows = length + 2
    shift = [(i, i + 1) for i in range(parts_count - 1)]
    halo = lax.ppermute(streams[row_count - halo_rows :], SEQ, shift)
    extended = jnp.concatenate([halo, streams], axis=0)
    gated = hyena_core(extended, conv_weight, table)
    partial_out = jnp.dot(gated, out_weight, preferred_element_type=jnp.float32)
    summed = lax.psum_scatter(
        partial_out.astype(jnp.bfloat16), "chan", scatter_dimension=1, tiled=True
    )
    return (tokens.astype(jnp.float32) + summed.astype(jnp.float32)).astype(jnp.bfloat16)


SEQ = ("x", "core")


def solution(mesh):
    seq_count, chan_count = mesh.devices.shape
    split = Mesh(mesh.devices.reshape(seq_count // 2, 2, chan_count), ("x", "core", "chan"))
    return jax.shard_map(
        local,
        mesh=split,
        in_specs=(
            P(SEQ, "chan"),
            P("chan"),
            P(SEQ, None, "chan"),
            P(None, None, "chan"),
            P("chan", None),
            P("chan", None),
        ),
        out_specs=P(SEQ, "chan"),
        check_vma=False,
    )
```

```python
import jax
import jax.numpy as jnp
import numpy as np
from jax import lax
from jax.sharding import Mesh, PartitionSpec as P


def lag_table(filters):
    groups, length = filters.shape
    width = 3 * length
    zeros = jnp.zeros((groups, length), filters.dtype)
    skew = jnp.concatenate([zeros, filters[:, ::-1], zeros], axis=1)
    tiled = jnp.tile(skew, (1, length))[:, : length * (width - 1)]
    rows = tiled.reshape(groups, length, width - 1)
    return rows[:, :, length - 1 : 3 * length - 1]


def hyena_core(extended, conv_weight, table):
    length = table.shape[1]
    values = extended.astype(jnp.float32)
    weights = conv_weight.astype(jnp.float32)
    shaped = (
        weights[:, 0, :] * values[2:]
        + weights[:, 1, :] * values[1:-1]
        + weights[:, 2, :] * values[:-2]
    )
    total = shaped.shape[0]
    out_rows = total - length
    query = shaped[length:, 0, :]
    mixed = (shaped[:, 1, :] * shaped[:, 2, :]).astype(jnp.bfloat16)
    group_count = table.shape[0]
    channel_count = mixed.shape[1]
    blocks = mixed.reshape(total // length, length, group_count, channel_count // group_count)
    paired = jnp.concatenate([blocks[:-1], blocks[1:]], axis=1)
    filtered = jnp.einsum(
        "gts,bsgw->btgw", table, paired, preferred_element_type=jnp.float32
    )
    filtered = filtered.reshape(out_rows, channel_count)
    return (query * filtered).astype(jnp.bfloat16)


def local(tokens, norm_gain, in_weight, conv_weight, filters, out_weight):
    row_count = tokens.shape[0]
    depth, _, chan_count = in_weight.shape
    length = filters.shape[1]
    joined = jnp.concatenate([tokens, norm_gain[None, :]], axis=0)
    whole_joined = lax.all_gather(joined, "chan", axis=1, tiled=True)
    table = lag_table(filters)
    table, whole_joined = lax.optimization_barrier((table, whole_joined))
    whole, gain_whole = whole_joined[:row_count], whole_joined[row_count]
    values = whole.astype(jnp.float32)
    mean_square = jnp.mean(values * values, axis=1, keepdims=True)
    normed = (values * lax.rsqrt(mean_square + 1e-06) * gain_whole.astype(jnp.float32)).astype(
        jnp.bfloat16
    )
    x_count = lax.axis_size("x")
    x_me = lax.axis_index("x")
    core_me = lax.axis_index("core")
    own = [in_weight]
    for k in range(1, x_count):
        own.append(lax.ppermute(in_weight, "x", [(i, (i + k) % x_count) for i in range(x_count)]))
    late = x_count // 2
    early = [k for k in range(x_count) if k != late]
    ordered = []
    for parity in (core_me, 1 - core_me):
        pieces = []
        for k in range(x_count):
            owner = 2 * lax.rem(x_me - k + x_count, x_count) + parity
            pieces.append(lax.dynamic_slice_in_dim(normed, owner * depth, depth, axis=1))
        ordered.append(jnp.concatenate([pieces[k] for k in early], axis=1))
        ordered.append(pieces[late])
    ordered = tuple(ordered)
    swap = [(0, 1), (1, 0)]
    forwarded = {0: lax.ppermute(own[0], "core", swap)}
    for k in early[1:]:
        block, ordered = lax.optimization_barrier((own[k], ordered))
        forwarded[k] = lax.ppermute(block, "core", swap)
    firsts, ordered, table = lax.optimization_barrier(
        (tuple(own[k] for k in early), ordered, table)
    )

    def joined_blocks(blocks):
        return jnp.concatenate([block.transpose(1, 0, 2) for block in blocks], axis=1)

    def product(rows, blocks):
        return jnp.einsum(
            "rk,ikc->ric", rows, joined_blocks(blocks), preferred_element_type=jnp.float32
        )

    projected = product(ordered[0], firsts)
    last, projected = lax.optimization_barrier((own[late], projected))
    forwarded[late] = lax.ppermute(last, "core", swap)
    projected, seconds = lax.optimization_barrier(
        (projected, tuple(forwarded[k] for k in early))
    )
    projected = projected + product(ordered[2], seconds)
    projected = projected + product(ordered[1], (last,))
    projected, second_last = lax.optimization_barrier((projected, forwarded[late]))
    projected = projected + product(ordered[3], (second_last,))
    streams = projected.astype(jnp.bfloat16)
    parts_count = lax.axis_size(SEQ)
    halo_rows = length + 2
    shift = [(i, i + 1) for i in range(parts_count - 1)]
    halo = lax.ppermute(streams[row_count - halo_rows :], SEQ, shift)
    extended = jnp.concatenate([halo, streams], axis=0)
    gated = hyena_core(extended, conv_weight, table)
    partial_out = jnp.dot(gated, out_weight, preferred_element_type=jnp.float32)
    summed = lax.psum_scatter(
        partial_out.astype(jnp.bfloat16), "chan", scatter_dimension=1, tiled=True
    )
    return (tokens.astype(jnp.float32) + summed.astype(jnp.float32)).astype(jnp.bfloat16)


SEQ = ("x", "core")


def solution(mesh):
    seq_count, chan_count = mesh.devices.shape
    split = Mesh(mesh.devices.reshape(seq_count // 2, 2, chan_count), ("x", "core", "chan"))
    return jax.shard_map(
        local,
        mesh=split,
        in_specs=(
            P(SEQ, "chan"),
            P("chan"),
            P(SEQ, None, "chan"),
            P(None, None, "chan"),
            P("chan", None),
            P("chan", None),
        ),
        out_specs=P(SEQ, "chan"),
        check_vma=False,
    )
```

```python
import jax
import jax.numpy as jnp
import numpy as np
from jax import lax
from jax.sharding import Mesh, PartitionSpec as P


def lag_table(filters):
    groups, length = filters.shape
    width = 3 * length
    zeros = jnp.zeros((groups, length), filters.dtype)
    skew = jnp.concatenate([zeros, filters[:, ::-1], zeros], axis=1)
    tiled = jnp.tile(skew, (1, length))[:, : length * (width - 1)]
    rows = tiled.reshape(groups, length, width - 1)
    return rows[:, :, length - 1 : 3 * length - 1]


def hyena_core(extended, conv_weight, table):
    length = table.shape[1]
    values = extended.astype(jnp.float32)
    weights = conv_weight.astype(jnp.float32)
    shaped = (
        weights[:, 0, :] * values[2:]
        + weights[:, 1, :] * values[1:-1]
        + weights[:, 2, :] * values[:-2]
    )
    total = shaped.shape[0]
    out_rows = total - length
    query = shaped[length:, 0, :]
    mixed = (shaped[:, 1, :] * shaped[:, 2, :]).astype(jnp.bfloat16)
    group_count = table.shape[0]
    channel_count = mixed.shape[1]
    blocks = mixed.reshape(total // length, length, group_count, channel_count // group_count)
    paired = jnp.concatenate([blocks[:-1], blocks[1:]], axis=1)
    filtered = jnp.einsum(
        "gts,bsgw->btgw", table, paired, preferred_element_type=jnp.float32
    )
    filtered = filtered.reshape(out_rows, channel_count)
    return (query * filtered).astype(jnp.bfloat16)


def local(tokens, norm_gain, in_weight, conv_weight, filters, out_weight):
    row_count = tokens.shape[0]
    depth, _, chan_count = in_weight.shape
    length = filters.shape[1]
    joined = jnp.concatenate([tokens, norm_gain[None, :]], axis=0)
    whole_joined = lax.all_gather(joined, "chan", axis=1, tiled=True)
    table = lag_table(filters)
    table, whole_joined = lax.optimization_barrier((table, whole_joined))
    whole, gain_whole = whole_joined[:row_count], whole_joined[row_count]
    values = whole.astype(jnp.float32)
    mean_square = jnp.mean(values * values, axis=1, keepdims=True)
    normed = (values * lax.rsqrt(mean_square + 1e-06) * gain_whole.astype(jnp.float32)).astype(
        jnp.bfloat16
    )
    x_count = lax.axis_size("x")
    x_me = lax.axis_index("x")
    core_me = lax.axis_index("core")
    own = [in_weight]
    for k in range(1, x_count):
        own.append(lax.ppermute(in_weight, "x", [(i, (i + k) % x_count) for i in range(x_count)]))
    late = x_count // 2
    early = [k for k in range(x_count) if k != late]
    ordered = []
    for parity in (core_me, 1 - core_me):
        pieces = []
        for k in range(x_count):
            owner = 2 * lax.rem(x_me - k + x_count, x_count) + parity
            pieces.append(lax.dynamic_slice_in_dim(normed, owner * depth, depth, axis=1))
        ordered.append(jnp.concatenate([pieces[k] for k in early], axis=1))
        ordered.append(pieces[late])
    ordered = tuple(ordered)
    swap = [(0, 1), (1, 0)]
    forwarded = {0: lax.ppermute(own[0], "core", swap)}
    for k in early[1:]:
        block, ordered = lax.optimization_barrier((own[k], ordered))
        forwarded[k] = lax.ppermute(block, "core", swap)
    firsts, ordered, table = lax.optimization_barrier(
        (tuple(own[k] for k in early), ordered, table)
    )

    def joined_blocks(blocks):
        return jnp.concatenate([block.transpose(1, 0, 2) for block in blocks], axis=1)

    def product(rows, blocks):
        return jnp.einsum(
            "rk,ikc->ric", rows, joined_blocks(blocks), preferred_element_type=jnp.float32
        )

    projected = product(ordered[0], firsts)
    projected, seconds = lax.optimization_barrier(
        (projected, tuple(forwarded[k] for k in early))
    )
    projected = projected + product(ordered[2], seconds)
    last, projected = lax.optimization_barrier((own[late], projected))
    forwarded[late] = lax.ppermute(last, "core", swap)
    projected = projected + product(ordered[1], (last,))
    projected, second_last = lax.optimization_barrier((projected, forwarded[late]))
    projected = projected + product(ordered[3], (second_last,))
    streams = projected.astype(jnp.bfloat16)
    parts_count = lax.axis_size(SEQ)
    halo_rows = length + 2
    shift = [(i, i + 1) for i in range(parts_count - 1)]
    halo = lax.ppermute(streams[row_count - halo_rows :], SEQ, shift)
    extended = jnp.concatenate([halo, streams], axis=0)
    gated = hyena_core(extended, conv_weight, table)
    partial_out = jnp.dot(gated, out_weight, preferred_element_type=jnp.float32)
    summed = lax.psum_scatter(
        partial_out.astype(jnp.bfloat16), "chan", scatter_dimension=1, tiled=True
    )
    return (tokens.astype(jnp.float32) + summed.astype(jnp.float32)).astype(jnp.bfloat16)


SEQ = ("x", "core")


def solution(mesh):
    seq_count, chan_count = mesh.devices.shape
    split = Mesh(mesh.devices.reshape(seq_count // 2, 2, chan_count), ("x", "core", "chan"))
    return jax.shard_map(
        local,
        mesh=split,
        in_specs=(
            P(SEQ, "chan"),
            P("chan"),
            P(SEQ, None, "chan"),
            P(None, None, "chan"),
            P("chan", None),
            P("chan", None),
        ),
        out_specs=P(SEQ, "chan"),
        check_vma=False,
    )
```

```python
import jax
import jax.numpy as jnp
import numpy as np
from jax import lax
from jax.sharding import Mesh, PartitionSpec as P


def lag_table(filters):
    groups, length = filters.shape
    width = 3 * length
    zeros = jnp.zeros((groups, length), filters.dtype)
    skew = jnp.concatenate([zeros, filters[:, ::-1], zeros], axis=1)
    tiled = jnp.tile(skew, (1, length))[:, : length * (width - 1)]
    rows = tiled.reshape(groups, length, width - 1)
    return rows[:, :, length - 1 : 3 * length - 1]


def hyena_core(extended, conv_weight, table):
    length = table.shape[1]
    values = extended.astype(jnp.float32)
    weights = conv_weight.astype(jnp.float32)
    shaped = (
        weights[:, 0, :] * values[2:]
        + weights[:, 1, :] * values[1:-1]
        + weights[:, 2, :] * values[:-2]
    )
    total = shaped.shape[0]
    out_rows = total - length
    query = shaped[length:, 0, :]
    mixed = (shaped[:, 1, :] * shaped[:, 2, :]).astype(jnp.bfloat16)
    group_count = table.shape[0]
    channel_count = mixed.shape[1]
    blocks = mixed.reshape(total // length, length, group_count, channel_count // group_count)
    paired = jnp.concatenate([blocks[:-1], blocks[1:]], axis=1)
    filtered = jnp.einsum(
        "gts,bsgw->btgw", table, paired, preferred_element_type=jnp.float32
    )
    filtered = filtered.reshape(out_rows, channel_count)
    return (query * filtered).astype(jnp.bfloat16)


def local(tokens, norm_gain, in_weight, conv_weight, filters, out_weight):
    row_count = tokens.shape[0]
    depth, _, chan_count = in_weight.shape
    length = filters.shape[1]
    joined = jnp.concatenate([tokens, norm_gain[None, :]], axis=0)
    whole_joined = lax.all_gather(joined, "chan", axis=1, tiled=True)
    table = lag_table(filters)
    table, whole_joined = lax.optimization_barrier((table, whole_joined))
    whole, gain_whole = whole_joined[:row_count], whole_joined[row_count]
    values = whole.astype(jnp.float32)
    mean_square = jnp.mean(values * values, axis=1, keepdims=True)
    normed = (values * lax.rsqrt(mean_square + 1e-06) * gain_whole.astype(jnp.float32)).astype(
        jnp.bfloat16
    )
    x_count = lax.axis_size("x")
    x_me = lax.axis_index("x")
    core_me = lax.axis_index("core")
    own = [in_weight]
    for k in range(1, x_count):
        own.append(lax.ppermute(in_weight, "x", [(i, (i + k) % x_count) for i in range(x_count)]))
    late = x_count // 2
    early = [k for k in range(x_count) if k != late]
    ordered = []
    for parity in (core_me, 1 - core_me):
        pieces = []
        for k in range(x_count):
            owner = 2 * lax.rem(x_me - k + x_count, x_count) + parity
            pieces.append(lax.dynamic_slice_in_dim(normed, owner * depth, depth, axis=1))
        ordered.append(jnp.concatenate([pieces[k] for k in early], axis=1))
        ordered.append(pieces[late])
    ordered = tuple(ordered)
    swap = [(0, 1), (1, 0)]
    forwarded = {0: lax.ppermute(own[0], "core", swap)}
    for k in early[1:]:
        block, ordered = lax.optimization_barrier((own[k], ordered))
        forwarded[k] = lax.ppermute(block, "core", swap)
    firsts, ordered, table = lax.optimization_barrier(
        (tuple(own[k] for k in early), ordered, table)
    )

    def joined_blocks(blocks):
        return jnp.concatenate([block.transpose(1, 0, 2) for block in blocks], axis=1)

    def product(rows, blocks):
        return jnp.einsum(
            "rk,ikc->ric", rows, joined_blocks(blocks), preferred_element_type=jnp.float32
        )

    projected = product(ordered[0], firsts)
    projected, seconds = lax.optimization_barrier(
        (projected, tuple(forwarded[k] for k in early))
    )
    projected = projected + product(ordered[2], seconds)
    last, projected = lax.optimization_barrier((own[late], projected))
    forwarded[late] = lax.ppermute(last, "core", swap)
    projected, second_last = lax.optimization_barrier((projected, forwarded[late]))
    tail_rows = jnp.concatenate([ordered[1], ordered[3]], axis=1)
    projected = projected + product(tail_rows, (last, second_last))
    streams = projected.astype(jnp.bfloat16)
    parts_count = lax.axis_size(SEQ)
    halo_rows = length + 2
    shift = [(i, i + 1) for i in range(parts_count - 1)]
    halo = lax.ppermute(streams[row_count - halo_rows :], SEQ, shift)
    extended = jnp.concatenate([halo, streams], axis=0)
    gated = hyena_core(extended, conv_weight, table)
    partial_out = jnp.dot(gated, out_weight, preferred_element_type=jnp.float32)
    summed = lax.psum_scatter(
        partial_out.astype(jnp.bfloat16), "chan", scatter_dimension=1, tiled=True
    )
    return (tokens.astype(jnp.float32) + summed.astype(jnp.float32)).astype(jnp.bfloat16)


SEQ = ("x", "core")


def solution(mesh):
    seq_count, chan_count = mesh.devices.shape
    split = Mesh(mesh.devices.reshape(seq_count // 2, 2, chan_count), ("x", "core", "chan"))
    return jax.shard_map(
        local,
        mesh=split,
        in_specs=(
            P(SEQ, "chan"),
            P("chan"),
            P(SEQ, None, "chan"),
            P(None, None, "chan"),
            P("chan", None),
            P("chan", None),
        ),
        out_specs=P(SEQ, "chan"),
        check_vma=False,
    )
```
